32 devices in a mesh: teacher: 4 (over y, x), vocab: 8 (over z, core).
Axes of the slice: x: 2, y: 2, z: 4, core: 2. Of those that a mesh axis runs over, the one named last changes fastest.
Arguments:
- teacher_hidden: bfloat16 [4, 1024, 4096], P('teacher', 'vocab'), may hold values from -180 to 180
- teacher_head: bfloat16 [4, 4096, 32000], P('teacher', None, 'vocab'), may hold values from -0.375 to 0.375
- student_hidden: bfloat16 [1024, 4096], P('teacher'), may hold values from -180 to 180
- student_head: bfloat16 [4096, 32000], P('teacher', 'vocab'), may hold values from -0.375 to 0.375
Outputs:
- loss: float32 [], replicated
- grad_hidden: float32 [1024, 4096], P('teacher', 'vocab')
- grad_weight: float32 [4096, 32000], P('teacher', 'vocab')
The draws below stay inside these ranges and needn't reach their ends.
All inputs are finite; a program needn't handle non-finite values.
Results may differ from the reference program's by a relative error of at most 0.0027.
Values may be sent and summed in bfloat16 or wider, within the bound.
A program may use at most 192 MiB of HBM per device.

```python
import jax
import jax.numpy as jnp
from jax import lax

D = 4096
V = 32000
TOK = 1024
TEACHERS = 4


def rows_draw(key, shape):
    first = jax.random.fold_in(key, 0)
    values = jax.random.normal(first, shape, jnp.float32)
    return jnp.clip(values, -180.0, 180.0)


def draw_teacher_hidden(key, part):
    return rows_draw(jax.random.fold_in(key, 17), (TEACHERS, TOK, D)).astype(jnp.bfloat16)


def draw_student_hidden(key, part):
    return rows_draw(jax.random.fold_in(key, 29), (TOK, D)).astype(jnp.bfloat16)


def level_of(key, extent, cuts, low, top_value):
    level = 1.0
    for axis_at, parts in cuts:
        draws = jax.random.uniform(jax.random.fold_in(jax.random.fold_in(key, 6), axis_at), (parts,), jnp.float32, low / len(cuts), top_value / len(cuts))
        level = level * jnp.repeat(jnp.exp(draws), extent[axis_at] // parts).reshape((-1,) + (1,) * (len(extent) - 1 - axis_at))
    return level


def bell_draw(stream_key, shape, deviation, most, pieces=(), dtype=jnp.bfloat16):
    level = level_of(stream_key, shape, pieces, -0.22, 0.18) if pieces else 1.0
    entries = jax.random.normal(stream_key, shape, jnp.float32) * deviation * level
    return jnp.minimum(jnp.maximum(entries, -most), most).astype(dtype)


def setup_inputs(seed: int = 0) -> dict:
    streams_of = jax.random.split(jax.random.key(seed), 5)
    teacher_hidden = draw_teacher_hidden(jax.random.fold_in(streams_of[4], 71), 0)
    teacher_head = bell_draw(streams_of[1], (TEACHERS, D, V), (D // 16) ** -0.5, 0.375, ((0, 4), (2, 8)))
    student_hidden = draw_student_hidden(jax.random.fold_in(streams_of[4], 71), 0)
    student_head = bell_draw(streams_of[3], (D, V), (D // 16) ** -0.5, 0.375, ((0, 4), (1, 8)))
    return {"teacher_hidden": teacher_hidden, "teacher_head": teacher_head, "student_hidden": student_hidden, "student_head": student_head}


def row_stats(values):
    top = jnp.max(values, axis=-1, keepdims=True)
    shifted = jnp.exp(values - top)
    return top[..., 0], jnp.sum(shifted, axis=-1), jnp.sum(shifted * values, axis=-1)


def reference(teacher_hidden, teacher_head, student_hidden, student_head):
    def one_teacher(carry, pair):
        hidden, head = pair
        logits = jnp.dot(hidden, head, preferred_element_type=jnp.float32)
        top, total, moment = row_stats(logits)
        lse = top + jnp.log(total)
        entropy = lse - moment / total
        confid = jnp.exp(-entropy)
        return (carry[0] + confid[:, None] * (logits - lse[:, None]), carry[1] + confid), None

    init = (jnp.zeros((TOK, V), jnp.float32), jnp.zeros((TOK,), jnp.float32))
    (wsum, csum), _ = lax.scan(one_teacher, init, (teacher_hidden, teacher_head))
    raw = wsum / csum[:, None]
    top, total, _ = row_stats(raw)
    target = raw - (top + jnp.log(total))[:, None]
    slog = jnp.dot(student_hidden, student_head, preferred_element_type=jnp.float32)
    top, total, _ = row_stats(slog)
    slp = slog - (top + jnp.log(total))[:, None]
    probs = jnp.exp(target)
    loss = jnp.sum(probs * (target - slp)) / TOK
    gradl = (jnp.exp(slp) - probs).astype(jnp.bfloat16)
    grad_hidden = jnp.dot(gradl, student_head.T, preferred_element_type=jnp.float32)
    grad_weight = jnp.dot(student_hidden.T, gradl, preferred_element_type=jnp.float32)
    return loss, grad_hidden, grad_weight
```

```python
import functools

import jax
import jax.numpy as jnp
from jax import lax
from jax.experimental import pallas as pl
from jax.experimental.pallas import tpu as pltpu
from jax.sharding import PartitionSpec as P

F32 = jnp.float32


def gather_hidden(own, nv, first):
    chips = nv // 2
    at = lax.axis_index("vocab")
    chip = at // 2
    up = [own]
    down = [own]
    for hop in range(chips - 1):
        up.append(lax.ppermute(up[-1], "vocab", [(i, i + 2) for i in range(nv - 2)]))
        down.append(lax.ppermute(down[-1], "vocab", [(i + 2, i) for i in range(nv - 2)]))
        if hop == 0:
            up[-1], down[-1], first = lax.optimization_barrier((up[-1], down[-1], first))
    pair = [(i, i ^ 1) for i in range(nv)]
    rows, width = own.shape
    buf = jnp.zeros((chips, 2, rows, width), own.dtype)
    core = at % 2
    for k in range(chips):
        piece = own if k == 0 else up[k] + down[chips - k]
        other = lax.ppermute(piece, "vocab", pair)
        slot = lax.rem(chip - k + chips, chips)
        buf = lax.dynamic_update_slice(buf, piece[None, None], (slot, core, 0, 0))
        buf = lax.dynamic_update_slice(buf, other[None, None], (slot, 1 - core, 0, 0))
    return buf.reshape(nv * rows, width), first


def exchange_kernel(nv, own_ref, out_ref, slots, send, recv):
    me = lax.axis_index("vocab")
    barrier = pltpu.get_barrier_semaphore()
    for step in range(1, nv):
        pl.semaphore_signal(
            barrier,
            inc=1,
            device_id={"vocab": lax.rem(me + step, nv)},
            device_id_type=pl.DeviceIdType.MESH,
        )
    pl.semaphore_wait(barrier, nv - 1)
    copies = []
    for step in range(1, nv):
        copies.append(
            pltpu.make_async_remote_copy(
                src_ref=own_ref,
                dst_ref=slots.at[me],
                send_sem=send.at[step - 1],
                recv_sem=recv.at[step - 1],
                device_id={"vocab": lax.rem(me + step, nv)},
                device_id_type=pl.DeviceIdType.MESH,
            )
        )
        copies[-1].start()
    slots[me] = own_ref[...]
    for copy in copies:
        copy.wait()
    out_ref[...] = slots[...]


def slotted(stats, nv, ident):
    return pl.pallas_call(
        functools.partial(exchange_kernel, nv),
        out_shape=jax.ShapeDtypeStruct((nv,) + stats.shape, F32),
        in_specs=[pl.BlockSpec(memory_space=pltpu.VMEM)],
        out_specs=pl.BlockSpec(memory_space=pltpu.VMEM),
        scratch_shapes=[
            pltpu.VMEM((nv,) + stats.shape, F32),
            pltpu.SemaphoreType.DMA((nv - 1,)),
            pltpu.SemaphoreType.DMA((nv - 1,)),
        ],
        compiler_params=pltpu.CompilerParams(collective_id=ident, has_side_effects=True),
    )(stats)


def per_device(nt, nv, tok, teacher_hidden, teacher_head, student_hidden, student_head):
    head = teacher_head[0]
    columns = lax.all_to_all(student_hidden, "teacher", split_axis=1, concat_axis=0, tiled=True)
    partial_slog = jnp.dot(columns, student_head, preferred_element_type=F32)
    hidden, partial_slog = gather_hidden(teacher_hidden[0], nv, partial_slog)
    slog = lax.psum_scatter(partial_slog, "teacher", scatter_dimension=0, tiled=True)

    logits = jnp.dot(hidden, head, preferred_element_type=F32)
    m = jnp.max(logits, axis=-1)
    e = jnp.exp(logits - m[:, None])
    st = slotted(jnp.stack([m, jnp.sum(e, axis=-1), jnp.sum(e * logits, axis=-1)]), nv, 0)
    top = jnp.max(st[:, 0], axis=0)
    scale = jnp.exp(st[:, 0] - top)
    total = jnp.sum(st[:, 1] * scale, axis=0)
    moment = jnp.sum(st[:, 2] * scale, axis=0)
    lse = top + jnp.log(total)
    confid = jnp.exp(moment / total - lse)
    weighted = confid[:, None] * (logits - lse[:, None])
    slog, weighted = lax.optimization_barrier((slog, weighted))
    wsum = lax.psum_scatter(weighted, "teacher", scatter_dimension=0, tiled=True)
    csum = lax.psum_scatter(confid, "teacher", scatter_dimension=0, tiled=True)

    raw = wsum / csum[:, None]
    ms = jnp.max(slog, axis=-1)
    ss = jnp.sum(jnp.exp(slog - ms[:, None]), axis=-1)
    mr = jnp.max(raw, axis=-1)
    er = jnp.exp(raw - mr[:, None])
    st = slotted(
        jnp.stack([mr, jnp.sum(er, axis=-1), jnp.sum(er * (raw - slog), axis=-1), ms, ss]), nv, 1
    )
    tr = jnp.max(st[:, 0], axis=0)
    cr = jnp.exp(st[:, 0] - tr)
    total_r = jnp.sum(st[:, 1] * cr, axis=0)
    cross = jnp.sum(st[:, 2] * cr, axis=0)
    ts = jnp.max(st[:, 3], axis=0)
    total_s = jnp.sum(st[:, 4] * jnp.exp(st[:, 3] - ts), axis=0)
    lse_r = tr + jnp.log(total_r)
    lse_s = ts + jnp.log(total_s)
    kl = cross / total_r - lse_r + lse_s
    gradl = (jnp.exp(slog - lse_s[:, None]) - jnp.exp(raw - lse_r[:, None])).astype(jnp.bfloat16)
    all_grads = lax.all_gather(gradl, "teacher", axis=0, tiled=True)
    loss = lax.psum(jnp.sum(kl), "teacher") / tok

    r = nv // nt
    feats = student_head.shape[0]
    gh = lax.dot_general(
        all_grads, student_head, (((1,), (1,)), ((), ())), preferred_element_type=F32
    )
    gh = gh.reshape(nt, tok // nt, r, feats // r).transpose(0, 2, 1, 3)
    gh = gh.reshape(nv * (tok // nt), feats // r)
    gh = lax.psum_scatter(gh, "vocab", scatter_dimension=0, tiled=True)
    swap = [
        (s * nv + t * r + c, t * nv + s * r + c)
        for s in range(nt)
        for t in range(nt)
        for c in range(r)
    ]
    grad_hidden = lax.ppermute(gh, ("teacher", "vocab"), swap)
    grad_weight = lax.dot_general(
        columns, all_grads, (((0,), (0,)), ((), ())), preferred_element_type=F32
    )
    return (loss, grad_hidden, grad_weight)


def solution(mesh):
    nt, nv = mesh.shape["teacher"], mesh.shape["vocab"]

    def whole(teacher_hidden, teacher_head, student_hidden, student_head):
        tok = student_hidden.shape[0]
        return jax.shard_map(
            lambda *a: per_device(nt, nv, tok, *a),
            mesh=mesh,
            in_specs=(
                P("teacher", "vocab", None),
                P("teacher", None, "vocab"),
                P("teacher", None),
                P("teacher", "vocab"),
            ),
            out_specs=(P(), P("teacher", "vocab"), P("teacher", "vocab")),
            check_vma=False,
        )(teacher_hidden, teacher_head, student_hidden, student_head)

    return whole
```

```python
import functools

import jax
import jax.numpy as jnp
from jax import lax
from jax.experimental import pallas as pl
from jax.experimental.pallas import tpu as pltpu
from jax.sharding import PartitionSpec as P

F32 = jnp.float32


def gather_hidden(own, nv, first):
    chips = nv // 2
    at = lax.axis_index("vocab")
    chip = at // 2
    up = [own]
    down = [own]
    for hop in range(chips - 1):
        up.append(lax.ppermute(up[-1], "vocab", [(i, i + 2) for i in range(nv - 2)]))
        down.append(lax.ppermute(down[-1], "vocab", [(i + 2, i) for i in range(nv - 2)]))
        if hop == 1:
            up[-1], down[-1], first = lax.optimization_barrier((up[-1], down[-1], first))
    pair = [(i, i ^ 1) for i in range(nv)]
    rows, width = own.shape
    buf = jnp.zeros((chips, 2, rows, width), own.dtype)
    core = at % 2
    for k in range(chips):
        piece = own if k == 0 else up[k] + down[chips - k]
        other = lax.ppermute(piece, "vocab", pair)
        slot = lax.rem(chip - k + chips, chips)
        buf = lax.dynamic_update_slice(buf, piece[None, None], (slot, core, 0, 0))
        buf = lax.dynamic_update_slice(buf, other[None, None], (slot, 1 - core, 0, 0))
    return buf.reshape(nv * rows, width), first


def exchange_kernel(nv, own_ref, out_ref, slots, send, recv):
    me = lax.axis_index("vocab")
    barrier = pltpu.get_barrier_semaphore()
    for step in range(1, nv):
        pl.semaphore_signal(
            barrier,
            inc=1,
            device_id={"vocab": lax.rem(me + step, nv)},
            device_id_type=pl.DeviceIdType.MESH,
        )
    pl.semaphore_wait(barrier, nv - 1)
    copies = []
    for step in range(1, nv):
        copies.append(
            pltpu.make_async_remote_copy(
                src_ref=own_ref,
                dst_ref=slots.at[me],
                send_sem=send.at[step - 1],
                recv_sem=recv.at[step - 1],
                device_id={"vocab": lax.rem(me + step, nv)},
                device_id_type=pl.DeviceIdType.MESH,
            )
        )
        copies[-1].start()
    slots[me] = own_ref[...]
    for copy in copies:
        copy.wait()
    out_ref[...] = slots[...]


def slotted(stats, nv, ident):
    return pl.pallas_call(
        functools.partial(exchange_kernel, nv),
        out_shape=jax.ShapeDtypeStruct((nv,) + stats.shape, F32),
        in_specs=[pl.BlockSpec(memory_space=pltpu.VMEM)],
        out_specs=pl.BlockSpec(memory_space=pltpu.VMEM),
        scratch_shapes=[
            pltpu.VMEM((nv,) + stats.shape, F32),
            pltpu.SemaphoreType.DMA((nv - 1,)),
            pltpu.SemaphoreType.DMA((nv - 1,)),
        ],
        compiler_params=pltpu.CompilerParams(collective_id=ident, has_side_effects=True),
    )(stats)


def per_device(nt, nv, tok, teacher_hidden, teacher_head, student_hidden, student_head):
    head = teacher_head[0]
    columns = lax.all_to_all(student_hidden, "teacher", split_axis=1, concat_axis=0, tiled=True)
    partial_slog = jnp.dot(columns, student_head, preferred_element_type=F32)
    hidden, partial_slog = gather_hidden(teacher_hidden[0], nv, partial_slog)
    slog = lax.psum_scatter(partial_slog, "teacher", scatter_dimension=0, tiled=True)

    logits = jnp.dot(hidden, head, preferred_element_type=F32)
    m = jnp.max(logits, axis=-1)
    e = jnp.exp(logits - m[:, None])
    st = slotted(jnp.stack([m, jnp.sum(e, axis=-1), jnp.sum(e * logits, axis=-1)]), nv, 0)
    top = jnp.max(st[:, 0], axis=0)
    scale = jnp.exp(st[:, 0] - top)
    total = jnp.sum(st[:, 1] * scale, axis=0)
    moment = jnp.sum(st[:, 2] * scale, axis=0)
    lse = top + jnp.log(total)
    confid = jnp.exp(moment / total - lse)
    weighted = confid[:, None] * (logits - lse[:, None])
    slog, weighted = lax.optimization_barrier((slog, weighted))
    wsum = lax.psum_scatter(weighted, "teacher", scatter_dimension=0, tiled=True)
    csum = lax.psum_scatter(confid, "teacher", scatter_dimension=0, tiled=True)

    raw = wsum / csum[:, None]
    ms = jnp.max(slog, axis=-1)
    ss = jnp.sum(jnp.exp(slog - ms[:, None]), axis=-1)
    mr = jnp.max(raw, axis=-1)
    er = jnp.exp(raw - mr[:, None])
    st = slotted(
        jnp.stack([mr, jnp.sum(er, axis=-1), jnp.sum(er * (raw - slog), axis=-1), ms, ss]), nv, 1
    )
    tr = jnp.max(st[:, 0], axis=0)
    cr = jnp.exp(st[:, 0] - tr)
    total_r = jnp.sum(st[:, 1] * cr, axis=0)
    cross = jnp.sum(st[:, 2] * cr, axis=0)
    ts = jnp.max(st[:, 3], axis=0)
    total_s = jnp.sum(st[:, 4] * jnp.exp(st[:, 3] - ts), axis=0)
    lse_r = tr + jnp.log(total_r)
    lse_s = ts + jnp.log(total_s)
    kl = cross / total_r - lse_r + lse_s
    gradl = (jnp.exp(slog - lse_s[:, None]) - jnp.exp(raw - lse_r[:, None])).astype(jnp.bfloat16)
    all_grads = lax.all_gather(gradl, "teacher", axis=0, tiled=True)
    loss = lax.psum(jnp.sum(kl), "teacher") / tok

    r = nv // nt
    feats = student_head.shape[0]
    gh = lax.dot_general(
        all_grads, student_head, (((1,), (1,)), ((), ())), preferred_element_type=F32
    )
    gh = lax.psum_scatter(gh, "vocab", scatter_dimension=0, tiled=True)
    grad_weight = lax.dot_general(
        columns, all_grads, (((0,), (0,)), ((), ())), preferred_element_type=F32
    )
    gh, grad_weight = lax.optimization_barrier((gh, grad_weight))
    part = lax.rem(lax.axis_index("vocab"), r)
    rows, width = gh.shape[0], feats // r
    grad_hidden = jnp.zeros((r, rows, width), F32)
    for k in range(r):
        swap = [
            (s * nv + t * r + h, t * nv + s * r + (h + k) % r)
            for s in range(nt)
            for t in range(nt)
            for h in range(r)
        ]
        piece = lax.dynamic_slice(gh, (0, lax.rem(part + k, r) * width), (rows, width))
        piece = lax.ppermute(piece, ("teacher", "vocab"), swap)
        grad_hidden = lax.dynamic_update_slice(
            grad_hidden, piece[None], (lax.rem(part + r - k, r), 0, 0)
        )
    grad_hidden = grad_hidden.reshape(r * rows, width)
    return (loss, grad_hidden, grad_weight)


def solution(mesh):
    nt, nv = mesh.shape["teacher"], mesh.shape["vocab"]

    def whole(teacher_hidden, teacher_head, student_hidden, student_head):
        tok = student_hidden.shape[0]
        return jax.shard_map(
            lambda *a: per_device(nt, nv, tok, *a),
            mesh=mesh,
            in_specs=(
                P("teacher", "vocab", None),
                P("teacher", None, "vocab"),
                P("teacher", None),
                P("teacher", "vocab"),
            ),
            out_specs=(P(), P("teacher", "vocab"), P("teacher", "vocab")),
            check_vma=False,
        )(teacher_hidden, teacher_head, student_hidden, student_head)

    return whole
```

```python
import functools

import jax
import jax.numpy as jnp
from jax import lax
from jax.experimental import pallas as pl
from jax.experimental.pallas import tpu as pltpu
from jax.sharding import PartitionSpec as P

F32 = jnp.float32


def gather_hidden(own, nv, first):
    chips = nv // 2
    at = lax.axis_index("vocab")
    chip = at // 2
    up = [own]
    down = [own]
    for hop in range(chips - 1):
        up.append(lax.ppermute(up[-1], "vocab", [(i, i + 2) for i in range(nv - 2)]))
        down.append(lax.ppermute(down[-1], "vocab", [(i + 2, i) for i in range(nv - 2)]))
        if hop == 1:
            up[-1], down[-1], first = lax.optimization_barrier((up[-1], down[-1], first))
    pair = [(i, i ^ 1) for i in range(nv)]
    rows, width = own.shape
    buf = jnp.zeros((chips, 2, rows, width), own.dtype)
    core = at % 2
    for k in range(chips):
        piece = own if k == 0 else up[k] + down[chips - k]
        other = lax.ppermute(piece, "vocab", pair)
        slot = lax.rem(chip - k + chips, chips)
        buf = lax.dynamic_update_slice(buf, piece[None, None], (slot, core, 0, 0))
        buf = lax.dynamic_update_slice(buf, other[None, None], (slot, 1 - core, 0, 0))
    return buf.reshape(nv * rows, width), first


def exchange_kernel(nv, own_ref, out_ref, slots, send, recv):
    me = lax.axis_index("vocab")
    barrier = pltpu.get_barrier_semaphore()
    for step in range(1, nv):
        pl.semaphore_signal(
            barrier,
            inc=1,
            device_id={"vocab": lax.rem(me + step, nv)},
            device_id_type=pl.DeviceIdType.MESH,
        )
    pl.semaphore_wait(barrier, nv - 1)
    copies = []
    for step in range(1, nv):
        copies.append(
            pltpu.make_async_remote_copy(
                src_ref=own_ref,
                dst_ref=slots.at[me],
                send_sem=send.at[step - 1],
                recv_sem=recv.at[step - 1],
                device_id={"vocab": lax.rem(me + step, nv)},
                device_id_type=pl.DeviceIdType.MESH,
            )
        )
        copies[-1].start()
    slots[me] = own_ref[...]
    for copy in copies:
        copy.wait()
    out_ref[...] = slots[...]


def slotted(stats, nv, ident):
    return pl.pallas_call(
        functools.partial(exchange_kernel, nv),
        out_shape=jax.ShapeDtypeStruct((nv,) + stats.shape, F32),
        in_specs=[pl.BlockSpec(memory_space=pltpu.VMEM)],
        out_specs=pl.BlockSpec(memory_space=pltpu.VMEM),
        scratch_shapes=[
            pltpu.VMEM((nv,) + stats.shape, F32),
            pltpu.SemaphoreType.DMA((nv - 1,)),
            pltpu.SemaphoreType.DMA((nv - 1,)),
        ],
        compiler_params=pltpu.CompilerParams(collective_id=ident, has_side_effects=True),
    )(stats)


def per_device(nt, nv, tok, teacher_hidden, teacher_head, student_hidden, student_head):
    head = teacher_head[0]
    columns = lax.all_to_all(student_hidden, "teacher", split_axis=1, concat_axis=0, tiled=True)
    partial_slog = jnp.dot(columns, student_head, preferred_element_type=F32)
    hidden, partial_slog = gather_hidden(teacher_hidden[0], nv, partial_slog)
    slog = lax.psum_scatter(partial_slog, "teacher", scatter_dimension=0, tiled=True)

    logits = jnp.dot(hidden, head, preferred_element_type=F32)
    m = jnp.max(logits, axis=-1)
    e = jnp.exp(logits - m[:, None])
    st = slotted(jnp.stack([m, jnp.sum(e, axis=-1), jnp.sum(e * logits, axis=-1)]), nv, 0)
    top = jnp.max(st[:, 0], axis=0)
    scale = jnp.exp(st[:, 0] - top)
    total = jnp.sum(st[:, 1] * scale, axis=0)
    moment = jnp.sum(st[:, 2] * scale, axis=0)
    lse = top + jnp.log(total)
    confid = jnp.exp(moment / total - lse)
    weighted = confid[:, None] * (logits - lse[:, None])
    slog, weighted = lax.optimization_barrier((slog, weighted))
    wsum = lax.psum_scatter(weighted, "teacher", scatter_dimension=0, tiled=True)
    csum = lax.psum_scatter(confid, "teacher", scatter_dimension=0, tiled=True)

    raw = wsum / csum[:, None]
    ms = jnp.max(slog, axis=-1)
    ss = jnp.sum(jnp.exp(slog - ms[:, None]), axis=-1)
    mr = jnp.max(raw, axis=-1)
    er = jnp.exp(raw - mr[:, None])
    st = slotted(
        jnp.stack([mr, jnp.sum(er, axis=-1), jnp.sum(er * (raw - slog), axis=-1), ms, ss]), nv, 1
    )
    tr = jnp.max(st[:, 0], axis=0)
    cr = jnp.exp(st[:, 0] - tr)
    total_r = jnp.sum(st[:, 1] * cr, axis=0)
    cross = jnp.sum(st[:, 2] * cr, axis=0)
    ts = jnp.max(st[:, 3], axis=0)
    total_s = jnp.sum(st[:, 4] * jnp.exp(st[:, 3] - ts), axis=0)
    lse_r = tr + jnp.log(total_r)
    lse_s = ts + jnp.log(total_s)
    kl = cross / total_r - lse_r + lse_s
    gradl = (jnp.exp(slog - lse_s[:, None]) - jnp.exp(raw - lse_r[:, None])).astype(jnp.bfloat16)
    all_grads = lax.all_gather(gradl, "teacher", axis=0, tiled=True)
    loss = lax.psum(jnp.sum(kl), "teacher") / tok
    all_grads, loss = lax.optimization_barrier((all_grads, loss))

    r = nv // nt
    feats = student_head.shape[0]
    gh = lax.dot_general(
        all_grads, student_head, (((1,), (1,)), ((), ())), preferred_element_type=F32
    )
    gh = lax.psum_scatter(gh, "vocab", scatter_dimension=0, tiled=True)
    grad_weight = lax.dot_general(
        columns, all_grads, (((0,), (0,)), ((), ())), preferred_element_type=F32
    )
    gh, grad_weight = lax.optimization_barrier((gh, grad_weight))
    part = lax.rem(lax.axis_index("vocab"), r)
    rows, width = gh.shape[0], feats // r
    grad_hidden = jnp.zeros((r, rows, width), F32)
    for k in range(r):
        swap = [
            (s * nv + t * r + h, t * nv + s * r + (h + k) % r)
            for s in range(nt)
            for t in range(nt)
            for h in range(r)
        ]
        piece = lax.dynamic_slice(gh, (0, lax.rem(part + k, r) * width), (rows, width))
        piece = lax.ppermute(piece, ("teacher", "vocab"), swap)
        grad_hidden = lax.dynamic_update_slice(
            grad_hidden, piece[None], (lax.rem(part + r - k, r), 0, 0)
        )
    grad_hidden = grad_hidden.reshape(r * rows, width)
    return (loss, grad_hidden, grad_weight)


def solution(mesh):
    nt, nv = mesh.shape["teacher"], mesh.shape["vocab"]

    def whole(teacher_hidden, teacher_head, student_hidden, student_head):
        tok = student_hidden.shape[0]
        return jax.shard_map(
            lambda *a: per_device(nt, nv, tok, *a),
            mesh=mesh,
            in_specs=(
                P("teacher", "vocab", None),
                P("teacher", None, "vocab"),
                P("teacher", None),
                P("teacher", "vocab"),
            ),
            out_specs=(P(), P("teacher", "vocab"), P("teacher", "vocab")),
            check_vma=False,
        )(teacher_hidden, teacher_head, student_hidden, student_head)

    return whole
```
